256 devices in a mesh: dp: 8 (over y, core), expert: 32 (over x, z).
Axes of the slice: x: 4, y: 4, z: 8, core: 2. Of those that a mesh axis runs over, the one named last changes fastest.
Arguments:
- tokens: bfloat16 [32768, 2048], P(('dp', 'expert')), may hold values from -6 to 6
- expert_ids: int32 [32768, 2], P(('dp', 'expert')), may hold values from 0 to 31, all different within a row; in each aligned block of 128 rows (0 to 127, 128 to 255, ...) at most 12 rows name the same one
- upstream: bfloat16 [32768, 2048], P(('dp', 'expert')), may hold values from -6 to 6
- gain: float32 [2048], replicated, may hold values from 0.5 to 1.5
- router: bfloat16 [2048, 32], replicated, may hold values from -0.125 to 0.125
- gate_weight_matrix: bfloat16 [32, 2048, 1024], P('expert', 'dp'), may hold values from -0.125 to 0.125
- up_weight: bfloat16 [32, 2048, 1024], P('expert', 'dp'), may hold values from -0.125 to 0.125
- down_weight: bfloat16 [32, 1024, 2048], P('expert', None, 'dp'), may hold values from -0.1875 to 0.1875
Outputs:
- mixed: bfloat16 [32768, 2048], P(('dp', 'expert'))
- d_tokens: bfloat16 [32768, 2048], P(('dp', 'expert'))
- gate_weight_gradient: bfloat16 [32, 2048, 1024], P('expert', 'dp')
- up_weight_gradient: bfloat16 [32, 2048, 1024], P('expert', 'dp')
- down_weight_gradient: bfloat16 [32, 1024, 2048], P('expert', None, 'dp')
- d_router: float32 [2048, 32], replicated
- d_gain: float32 [2048], replicated
The draws below stay inside these ranges and needn't reach their ends.
Inputs may be any that keep to these rules, and one draw needn't show every extreme that they name: `expert_ids`: the two experts of a token differ. Among the tokens of one device (aligned blocks of 128 rows) no expert is named more than 12 times, and in some block one expert is named exactly 12 times.
All inputs are finite; a program needn't handle non-finite values.
Results may differ from the reference program's by a relative error of at most 0.014.
Values may be sent and summed in bfloat16 or wider, within the bound.
No kernel may reach another device: no remote copies, remote signals or barrier semaphores. Data moves between devices by JAX's collectives and lax.ppermute only.
A program may use at most 128 MiB of HBM per device.

```python
import math
from functools import partial
import jax
import jax.numpy as jnp
import numpy as np
from jax import lax

D = 2048
FE = 1024
TOK_DEV = 128
EXPERT_TOTAL = 32
ROUTE_CEILING = 12
TOKENS = 32768
N_DP = 8
N_EXPERT = 32


def steps_of(stream_key, dims, pieces, smallest, top_value):
    factor_of = 1.0
    for dim, parts in pieces:
        heights = jax.random.uniform(jax.random.fold_in(jax.random.fold_in(stream_key, 6), dim), (parts,), jnp.float32, smallest / len(pieces), top_value / len(pieces))
        factor_of = factor_of * jnp.repeat(jnp.exp(heights), dims[dim] // parts).reshape((-1,) + (1,) * (len(dims) - 1 - dim))
    return factor_of


def assign_block(stream_key, own, number, rows, count, top, most, slope):
    sequence = jax.random.permutation(stream_key, count)
    packed, common = load_shares(count, rows * top, most, slope, True), load_shares(count, rows * top, most, slope, False)
    places = jnp.arange(count)

    def named(tallies, rotation):
        used = int((tallies > 0).sum())
        fixed = max(1, used // 4)
        passed = fixed + (places - fixed + rotation * (used - fixed)) % max(1, count - fixed)
        return jnp.zeros((count,), jnp.int32).at[sequence[jnp.where(places < fixed, places, passed)]].set(jnp.asarray(tallies, jnp.int32))

    tallies = jnp.where(number % 4 == 0, named(packed, number // 4), named(common, number - number // 4 - 1))
    mixed = jax.random.permutation(jax.random.fold_in(own, 3), count)
    giver, receiver = mixed[0:count // 2 * 2:2], mixed[1:count // 2 * 2:2]
    slack = jnp.minimum(tallies[giver] - 1, most - tallies[receiver]) // 2
    slack = jnp.where((giver == sequence[0]) | (receiver == sequence[0]) | (tallies[receiver] == 0), 0, jnp.maximum(slack, 0))
    passed = jax.random.randint(jax.random.fold_in(own, 4), (count // 2,), 0, 1 << 20) % (slack + 1)
    tallies = tallies.at[giver].add(-passed).at[receiver].add(passed)
    members = jnp.searchsorted(jnp.cumsum(tallies), jnp.arange(rows * top), side="right").astype(jnp.int32)
    listing = members.reshape(top, rows).T
    listing = listing[jax.random.permutation(jax.random.fold_in(own, 1), rows)]
    rotation = jax.random.randint(jax.random.fold_in(own, 2), (rows, 1), 0, top)
    return jnp.take_along_axis(listing, (jnp.arange(top)[None, :] + rotation) % top, axis=1)


def load_shares(number_of, total, bound, skew, full):
    weights = [(1 << 20) // math.isqrt(rank ** skew) + 1 for rank in range(1, number_of + 1)]
    largest = bound if full else min(bound, max(-(-total // number_of), total * weights[0] // sum(weights)))
    least = 1 if total - largest >= number_of - 1 else 0
    given, rest = [largest] + [least] * (number_of - 1), total - largest - least * (number_of - 1)
    while rest > 0:
        candidates = [i for i in range(1, number_of) if given[i] < largest] or [i for i in range(1, number_of) if given[i] < bound]
        pool, remaining = sum([weights[i] for i in candidates]), rest
        for i in candidates:
            addition = min(bound - given[i], max(1, remaining * weights[i] // pool), rest)
            given[i] = given[i] + addition
            rest = rest - addition
    return np.array(given)


def centred(stream_key, shape, scale, reach, pieces=(), kind=jnp.bfloat16):
    result = scale * jax.random.normal(stream_key, shape, jnp.float32)
    if pieces:
        result = result * steps_of(stream_key, shape, pieces, -0.22, 0.18)
    return jnp.clip(result, -reach, reach).astype(kind)


def setup_inputs(seed: int = 0) -> dict:
    keys = jax.random.split(jax.random.key(seed), 9)
    tokens = centred(keys[0], (TOKENS, D), 1.0, 6.0, ((0, 256),))
    expert_ids_keys = jax.random.split(jax.random.fold_in(keys[1], 1), TOKENS // TOK_DEV)
    expert_ids_turns = jax.random.permutation(jax.random.fold_in(keys[1], 3), TOKENS // TOK_DEV)
    expert_ids = jax.vmap(lambda own, number: assign_block(jax.random.fold_in(keys[1], 2), own, number, TOK_DEV, EXPERT_TOTAL, 2, ROUTE_CEILING, 2))(expert_ids_keys, expert_ids_turns).reshape((TOKENS, 2))
    upstream = centred(keys[2], (TOKENS, D), 1.0, 6.0, ((0, 256),))
    gain = jnp.clip(1.0 + 0.1 * jax.random.normal(keys[3], (D,), jnp.float32), 0.5, 1.5)
    router = centred(keys[4], (D, EXPERT_TOTAL), D ** -0.5, 0.125)
    gate_weight_matrix = centred(keys[5], (EXPERT_TOTAL, D, FE), D ** -0.5, 0.125, ((0, 32), (1, 8)))
    up_weight = centred(keys[6], (EXPERT_TOTAL, D, FE), D ** -0.5, 0.125, ((0, 32), (1, 8)))
    down_weight = centred(keys[7], (EXPERT_TOTAL, FE, D), FE ** -0.5, 0.1875, ((0, 32), (2, 8)))
    return {"tokens": tokens, "expert_ids": expert_ids, "upstream": upstream, "gain": gain, "router": router, "gate_weight_matrix": gate_weight_matrix, "up_weight": up_weight, "down_weight": down_weight}


norm_eps = 1e-06

def slot_layout(expert_ids, experts, capacity):
    flattened = expert_ids.reshape(-1)
    onehot = (flattened[:, None] == jnp.arange(experts, dtype=jnp.int32)[None, :]).astype(jnp.int32)
    ranking = lax.optimization_barrier(jnp.sum(jnp.cumsum(onehot, axis=0) * onehot, axis=1)) - 1
    slot_ids = (flattened * capacity + ranking).astype(jnp.int32)
    sources = jnp.zeros((experts * capacity,), jnp.int32).at[slot_ids].set(jnp.arange(flattened.shape[0], dtype=jnp.int32))
    counts = lax.optimization_barrier(jnp.sum(onehot, axis=0))
    slots_occupied = (jnp.arange(capacity, dtype=jnp.int32)[None, :] < counts[:, None]).reshape(-1)
    return (slot_ids, sources, slots_occupied)

def group_sum(left, right):
    left_groups = left.astype(jnp.float32).reshape(N_DP, -1, left.shape[1])
    right_groups = right.astype(jnp.float32).reshape(N_DP, -1, right.shape[1])
    partial_sums = jnp.einsum('pra,prb->pab', left_groups, right_groups).astype(jnp.bfloat16)
    partial_sums = lax.optimization_barrier(partial_sums)
    return lax.optimization_barrier(jnp.sum(partial_sums.astype(jnp.float32), axis=0)).astype(jnp.bfloat16)

def reference(tokens, expert_ids, upstream, gain, router, gate_weight_matrix, up_weight, down_weight):
    source = tokens.astype(jnp.float32)
    inverse = lax.rsqrt(lax.optimization_barrier(jnp.mean(source * source, axis=-1, keepdims=True)) + norm_eps)
    unit_rows = source * inverse
    normed = (unit_rows * gain).astype(jnp.bfloat16)
    scores = jax.nn.sigmoid(jnp.dot(normed, router, preferred_element_type=jnp.float32))
    picked = expert_ids[:, :, None] == jnp.arange(EXPERT_TOTAL, dtype=jnp.int32)[None, None, :]
    chosen = lax.optimization_barrier(jnp.sum(jnp.where(picked, scores[:, None, :], 0.0), axis=2))
    total = lax.optimization_barrier(jnp.sum(chosen, axis=1, keepdims=True))
    gates = chosen / total
    device_list = N_DP * N_EXPERT
    per_device = expert_ids.reshape(device_list, TOK_DEV, 2)
    layout = jax.vmap(partial(slot_layout, experts=EXPERT_TOTAL, capacity=ROUTE_CEILING))
    slot_ids, sources, slots_occupied = layout(per_device)
    offsets = (jnp.arange(device_list, dtype=jnp.int32) * (2 * TOK_DEV))[:, None]
    expert_allotted = (sources + offsets).astype(jnp.int32)
    expert_allotted = expert_allotted.reshape(device_list, EXPERT_TOTAL, ROUTE_CEILING).transpose(1, 0, 2).reshape(EXPERT_TOTAL, device_list * ROUTE_CEILING)
    row_alive_mask = slots_occupied.reshape(device_list, EXPERT_TOTAL, ROUTE_CEILING).transpose(1, 0, 2).reshape(EXPERT_TOTAL, device_list * ROUTE_CEILING).astype(jnp.float32)
    gate_flat = gates.reshape(-1)
    cotangent = upstream.astype(jnp.float32)

    def single_expert(carry, inputs):
        mixture_running, backward_running, gate_gradient_running = carry
        routes, live_rows, gate_w, up_w, down_w = inputs
        token_rows = routes // 2
        rows = normed[token_rows] * live_rows[:, None].astype(jnp.bfloat16)
        pre_gate = jnp.dot(rows, gate_w, preferred_element_type=jnp.float32)
        pre_up = jnp.dot(rows, up_w, preferred_element_type=jnp.float32)
        sigma = jax.nn.sigmoid(pre_gate)
        active = pre_gate * sigma
        hidden = (active * pre_up).astype(jnp.bfloat16)
        expert_out = jnp.dot(hidden, down_w, preferred_element_type=jnp.float32).astype(jnp.bfloat16)
        weight = gate_flat[routes] * live_rows
        cot_rows = cotangent[token_rows]
        d_out = (weight[:, None] * cot_rows).astype(jnp.bfloat16)
        dgate_rows = lax.optimization_barrier(jnp.sum(cot_rows * expert_out.astype(jnp.float32), axis=1)) * live_rows
        d_hidden = jnp.dot(d_out, down_w.T, preferred_element_type=jnp.float32)
        d_pre_gate = (d_hidden * pre_up * sigma * (1.0 + pre_gate * (1.0 - sigma))).astype(jnp.bfloat16)
        d_pre_up = (d_hidden * active).astype(jnp.bfloat16)
        d_rows = (jnp.dot(d_pre_gate, gate_w.T, preferred_element_type=jnp.float32) + jnp.dot(d_pre_up, up_w.T, preferred_element_type=jnp.float32)).astype(jnp.bfloat16)
        mixture_running = mixture_running.at[token_rows].add(weight[:, None] * expert_out.astype(jnp.float32))
        backward_running = backward_running.at[token_rows].add(d_rows.astype(jnp.float32) * live_rows[:, None])
        gate_gradient_running = gate_gradient_running.at[routes].add(dgate_rows)
        grads = (group_sum(rows, d_pre_gate), group_sum(rows, d_pre_up), group_sum(hidden, d_out))
        return ((mixture_running, backward_running, gate_gradient_running), grads)
    begin_offset = (jnp.zeros((TOKENS, D), jnp.float32), jnp.zeros((TOKENS, D), jnp.float32), jnp.zeros((TOKENS * 2,), jnp.float32))
    (mixture_running, backward_running, gate_gradient_running), (gate_weight_gradient, up_weight_gradient, down_weight_gradient) = lax.scan(single_expert, begin_offset, (expert_allotted, row_alive_mask, gate_weight_matrix, up_weight, down_weight))
    mixed = (source + mixture_running).astype(jnp.bfloat16)
    d_gates = gate_gradient_running.reshape(TOKENS, 2)
    blended = lax.optimization_barrier(jnp.sum(gates * d_gates, axis=1, keepdims=True))
    d_chosen = (d_gates - blended) / total
    d_logit = d_chosen * chosen * (1.0 - chosen)
    d_logits = lax.optimization_barrier(jnp.sum(jnp.where(picked, d_logit[:, :, None], 0.0), axis=1))
    router_float = router.astype(jnp.float32)
    d_normed = backward_running + jnp.dot(d_logits, router_float.T, precision=lax.Precision.HIGHEST)
    d_unit = d_normed * gain
    inner = lax.optimization_barrier(jnp.mean(d_unit * unit_rows, axis=-1, keepdims=True))
    d_tokens = (cotangent + inverse * (d_unit - unit_rows * inner)).astype(jnp.bfloat16)
    d_router = jnp.dot(normed.astype(jnp.float32).T, d_logits, precision=lax.Precision.HIGHEST)
    d_gain = lax.optimization_barrier(jnp.sum(d_normed * unit_rows, axis=0))
    return (mixed, d_tokens, gate_weight_gradient, up_weight_gradient, down_weight_gradient, d_router, d_gain)
```

```python
import jax
import jax.numpy as jnp
from jax import lax
from jax.sharding import PartitionSpec as P

norm_eps = 1e-06
f32 = jnp.float32
bf16 = jnp.bfloat16


def dot(left, right, dims, **options):
    return lax.dot_general(
        left, right, (dims, ((), ())), preferred_element_type=f32, **options
    )


def exchange(rows, experts):
    count, width = rows.shape
    packed = rows.reshape(experts, count // experts, width // 128, 128)
    moved = lax.all_to_all(packed, "expert", split_axis=0, concat_axis=0, tiled=True)
    return moved.reshape(count, width)


def on_device(
    tokens, expert_ids, upstream, gain, router, gate_weight_matrix, up_weight, down_weight
):
    experts = lax.axis_size("expert")
    tok_rows, width = tokens.shape
    capacity = 3 * tok_rows // experts
    slots = experts * capacity

    gate_full = lax.all_gather(gate_weight_matrix[0], "dp", axis=0, tiled=True)
    up_full = lax.all_gather(up_weight[0], "dp", axis=0, tiled=True)
    down_full = lax.all_gather(down_weight[0], "dp", axis=1, tiled=True)

    columns = jnp.arange(experts, dtype=jnp.int32)
    picked = expert_ids[:, :, None] == columns[None, None, :]
    named = (picked[:, 0] | picked[:, 1]).astype(bf16)
    order = jnp.arange(tok_rows, dtype=jnp.int32)
    earlier = (order[None, :] < order[:, None]).astype(bf16)
    ranks = dot(earlier, named, ((1,), (0,))).astype(jnp.int32)
    place = columns[None, :] * capacity + ranks
    slot_pairs = jnp.sum(jnp.where(picked, place[:, None, :], 0), axis=2)
    slot_of = jnp.arange(slots, dtype=jnp.int32)
    first = slot_of[None, :] == slot_pairs[:, :1]
    second = slot_of[None, :] == slot_pairs[:, 1:]
    take_first = first.astype(bf16)
    take_second = second.astype(bf16)
    spread = (first | second).astype(bf16)

    source = tokens.astype(f32)
    inverse = lax.rsqrt(jnp.mean(source * source, axis=-1, keepdims=True) + norm_eps)
    unit_rows = source * inverse
    normed = (unit_rows * gain).astype(bf16)
    send_rows = dot(spread, normed, ((0,), (0,))).astype(bf16)
    expert_in = exchange(send_rows, experts)

    scores = jax.nn.sigmoid(jnp.dot(normed, router, preferred_element_type=f32))
    chosen = jnp.sum(jnp.where(picked, scores[:, None, :], 0.0), axis=2)
    total = jnp.sum(chosen, axis=1, keepdims=True)
    gates = chosen / total
    slot_gates = jnp.sum(
        jnp.where(first, gates[:, :1], 0.0) + jnp.where(second, gates[:, 1:], 0.0), axis=0
    )
    cot_rows = dot(spread, upstream, ((0,), (0,)))
    d_send = (slot_gates[:, None] * cot_rows).astype(bf16)
    d_send, expert_in = lax.optimization_barrier((d_send, expert_in))
    d_out = exchange(d_send, experts)

    pre_gate = dot(expert_in, gate_full, ((1,), (0,)))
    pre_up = dot(expert_in, up_full, ((1,), (0,)))
    sigma = jax.nn.sigmoid(pre_gate)
    active = pre_gate * sigma
    hidden = (active * pre_up).astype(bf16)
    expert_out = dot(hidden, down_full, ((1,), (0,))).astype(bf16)
    returned = exchange(expert_out, experts)

    d_out, hidden, expert_out = lax.optimization_barrier((d_out, hidden, expert_out))
    down_part = dot(d_out, hidden, ((0,), (0,))).astype(bf16)
    d_down = lax.psum_scatter(down_part, "dp", scatter_dimension=0, tiled=True)
    d_out, down_part = lax.optimization_barrier((d_out, down_part))
    d_hidden = dot(d_out, down_full, ((1,), (1,)))
    d_pre_gate = (d_hidden * pre_up * sigma * (1.0 + pre_gate * (1.0 - sigma))).astype(bf16)
    d_pre_up = (d_hidden * active).astype(bf16)
    d_rows = (
        dot(d_pre_gate, gate_full, ((1,), (1,))) + dot(d_pre_up, up_full, ((1,), (1,)))
    ).astype(bf16)
    d_back = exchange(d_rows, experts)
    d_pre_gate, d_pre_up, d_rows = lax.optimization_barrier((d_pre_gate, d_pre_up, d_rows))
    d_gate = lax.psum_scatter(
        dot(expert_in, d_pre_gate, ((0,), (0,))).astype(bf16),
        "dp",
        scatter_dimension=0,
        tiled=True,
    )
    d_up = lax.psum_scatter(
        dot(expert_in, d_pre_up, ((0,), (0,))).astype(bf16),
        "dp",
        scatter_dimension=0,
        tiled=True,
    )
    gain_rows = jnp.sum(d_rows.astype(f32) * expert_in.astype(f32), axis=0) / gain

    cotangent = upstream.astype(f32)
    out_first = dot(take_first, returned, ((1,), (0,)))
    out_second = dot(take_second, returned, ((1,), (0,)))
    mixed = (source + gates[:, :1] * out_first + gates[:, 1:] * out_second).astype(bf16)
    d_gates = jnp.concatenate(
        [
            jnp.sum(cotangent * out_first, axis=1, keepdims=True),
            jnp.sum(cotangent * out_second, axis=1, keepdims=True),
        ],
        axis=1,
    )
    blended = jnp.sum(gates * d_gates, axis=1, keepdims=True)
    d_chosen = (d_gates - blended) / total
    d_logit = d_chosen * chosen * (1.0 - chosen)
    d_logits = jnp.sum(jnp.where(picked, d_logit[:, :, None], 0.0), axis=1)
    d_scored = dot(
        d_logits, router.astype(f32), ((1,), (1,)), precision=lax.Precision.HIGHEST
    )

    part_router = dot(
        d_logits, normed.astype(f32), ((0,), (0,)), precision=lax.Precision.HIGHEST
    )
    part_gain = gain_rows + jnp.sum(d_scored * unit_rows, axis=0)
    piece = width // experts
    parts = jnp.concatenate(
        [part_router, jnp.pad(part_gain.reshape(experts, piece), ((0, 0), (0, 128 - piece)))],
        axis=1,
    )
    mine = lax.all_to_all(parts[:, None], "expert", split_axis=0, concat_axis=0, tiled=True)
    mine = lax.psum(jnp.sum(mine, axis=0), "dp")
    every = lax.all_to_all(
        jnp.broadcast_to(mine[None], (experts,) + mine.shape),
        "expert",
        split_axis=0,
        concat_axis=0,
        tiled=True,
    )[:, 0]
    d_back, every = lax.optimization_barrier((d_back, every))
    d_router = every[:, :width].T
    d_gain = every[:, width : width + piece].reshape(width)

    spread_all = dot(spread, d_back, ((1,), (0,)))
    d_normed = spread_all + d_scored
    d_unit = d_normed * gain
    inner = jnp.mean(d_unit * unit_rows, axis=-1, keepdims=True)
    d_tokens = (cotangent + inverse * (d_unit - unit_rows * inner)).astype(bf16)
    return (
        mixed,
        d_tokens,
        d_gate[None],
        d_up[None],
        d_down.T[None],
        d_router,
        d_gain,
    )


def solution(mesh):
    return jax.shard_map(
        on_device,
        mesh=mesh,
        in_specs=(
            P(("dp", "expert"), None),
            P(("dp", "expert"), None),
            P(("dp", "expert"), None),
            P(),
            P(),
            P("expert", "dp", None),
            P("expert", "dp", None),
            P("expert", None, "dp"),
        ),
        out_specs=(
            P(("dp", "expert"), None),
            P(("dp", "expert"), None),
            P("expert", "dp", None),
            P("expert", "dp", None),
            P("expert", None, "dp"),
            P(),
            P(),
        ),
        check_vma=False,
    )
```

```python
import jax
import jax.numpy as jnp
from jax import lax
from jax.experimental import pallas as pl
from jax.experimental.pallas import tpu as pltpu
from jax.sharding import PartitionSpec as P

norm_eps = 1e-06
f32 = jnp.float32
bf16 = jnp.bfloat16
ALONG_X = 4
ALONG_Z = 8
HIGHEST = lax.Precision.HIGHEST


def dot(left, right, dims, **options):
    return lax.dot_general(
        left, right, (dims, ((), ())), preferred_element_type=f32, **options
    )


def pack(rows, experts):
    count, width = rows.shape
    return rows.reshape(experts, count // experts, width // 128, 128)


def unpack(packed):
    return packed.reshape(packed.shape[0] * packed.shape[1], -1)


def exchange(packed, after=None):
    if after is not None:
        packed = lax.optimization_barrier((packed, after))[0]
    return lax.all_to_all(packed, "expert", split_axis=0, concat_axis=0, tiled=True)


def shift_dp(value, step):
    count = lax.axis_size("dp")
    return lax.ppermute(value, "dp", [(i, (i + step) % count) for i in range(count)])


def flip_dp(value, bit):
    count = lax.axis_size("dp")
    return lax.ppermute(value, "dp", [(i, i ^ bit) for i in range(count)])


def shift_expert(value, along_x, along_z):
    pairs = []
    for x in range(ALONG_X):
        for z in range(ALONG_Z):
            there = (x + along_x) % ALONG_X * ALONG_Z + (z + along_z) % ALONG_Z
            pairs.append((x * ALONG_Z + z, there))
    return lax.ppermute(value, "expert", pairs)


def gather_by_permutes(block):
    count = lax.axis_size("dp")
    me = lax.axis_index("dp").astype(jnp.uint32)
    rows = block.shape[0]
    half = rows // 2
    before = shift_dp(block, 2)
    after = shift_dp(block, -2)
    far_top = shift_dp(before[:half], 2)
    far_low = shift_dp(after[half:], -2)
    pieces = [
        (block, me, 0),
        (before, me + (count - 2), 0),
        (after, me + 2, 0),
        (far_top, me + 4, 0),
        (far_low, me + 4, half),
    ]
    full = jnp.zeros((count * rows, block.shape[1]), block.dtype)
    for piece, owner, low in pieces:
        for value, index in ((piece, owner), (flip_dp(piece, 1), owner ^ 1)):
            start = (index & (count - 1)) * rows + low
            full = lax.dynamic_update_slice(full, value, (start, jnp.uint32(0)))
    return full


def weights_kernel(rows_ref, out_ref, gate_ref, up_ref, hidden_ref, grads_ref, columns_ref):
    @pl.when(pl.program_id(0) == 0)
    def _():
        columns_ref[...] = hidden_ref[...].T

    feed = gate_ref.shape[1]
    part = out_ref.shape[1]
    rows = rows_ref[...]
    rows = rows.T
    out = out_ref[...]

    @pl.loop(0, feed // part)
    def _(i):
        at = pl.ds(pl.multiple_of(i * part, part), part)
        grads_ref[:, at] = dot(rows, gate_ref[:, at], ((1,), (0,))).astype(bf16)
        at_up = pl.ds(pl.multiple_of(feed + i * part, part), part)
        grads_ref[:, at_up] = dot(rows, up_ref[:, at], ((1,), (0,))).astype(bf16)
        at_down = pl.ds(pl.multiple_of(2 * feed + i * part, part), part)
        grads_ref[:, at_down] = dot(columns_ref[at, :], out, ((1,), (0,))).astype(bf16)


def weight_gradients(rows, d_out, d_gate, d_up, hidden, parts):
    count, width = rows.shape
    feed = d_gate.shape[1]
    part = width // parts
    whole = pl.BlockSpec((count, feed), lambda p: (0, 0))
    return pl.pallas_call(
        weights_kernel,
        grid=(parts,),
        in_specs=[
            pl.BlockSpec((count, part), lambda p: (0, p)),
            pl.BlockSpec((count, part), lambda p: (0, p)),
            whole,
            whole,
            whole,
        ],
        scratch_shapes=[pltpu.VMEM((feed, count), bf16)],
        out_specs=pl.BlockSpec((part, 3 * feed), lambda p: (p, 0)),
        out_shape=jax.ShapeDtypeStruct((width, 3 * feed), bf16),
        cost_estimate=pl.CostEstimate(
            flops=6 * count * width * feed,
            bytes_accessed=2 * (3 * width * feed + 2 * count * width + 3 * count * feed),
            transcendentals=0,
        ),
        name="weight_gradients",
    )(rows, d_out, d_gate, d_up, hidden)


def body(
    tokens, expert_ids, upstream, gain, router, gate_weight_matrix, up_weight, down_weight
):
    experts = lax.axis_size("expert")
    shards = lax.axis_size("dp")
    me = lax.axis_index("expert").astype(jnp.uint32)
    my_x, my_z = me >> 3, me & (ALONG_Z - 1)
    tok_rows, width = tokens.shape
    feed = gate_weight_matrix.shape[2]
    capacity = 3 * tok_rows // experts
    slots = experts * capacity

    gate_full = lax.all_gather(gate_weight_matrix[0], "dp", axis=0, tiled=True)
    down_full = lax.all_gather(down_weight[0], "dp", axis=1, tiled=True)
    up_full = gather_by_permutes(up_weight[0])

    columns = jnp.arange(experts, dtype=jnp.int32)
    picked = expert_ids[:, :, None] == columns[None, None, :]
    named = (picked[:, 0] | picked[:, 1]).astype(bf16)
    order = jnp.arange(tok_rows, dtype=jnp.int32)
    earlier = (order[None, :] < order[:, None]).astype(bf16)
    ranks = dot(earlier, named, ((1,), (0,))).astype(jnp.int32)
    place = columns[None, :] * capacity + ranks
    slot_pairs = jnp.sum(jnp.where(picked, place[:, None, :], 0), axis=2)
    slot_of = jnp.arange(slots, dtype=jnp.int32)
    first = slot_of[None, :] == slot_pairs[:, :1]
    second = slot_of[None, :] == slot_pairs[:, 1:]
    take_first = first.astype(bf16)
    take_second = second.astype(bf16)
    spread = (first | second).astype(bf16)

    source = tokens.astype(f32)
    inverse = lax.rsqrt(jnp.mean(source * source, axis=-1, keepdims=True) + norm_eps)
    unit_rows = source * inverse
    normed = (unit_rows * gain).astype(bf16)
    send_rows = dot(spread, normed, ((0,), (0,))).astype(bf16)
    moved_in = exchange(pack(send_rows, experts))
    expert_in = unpack(moved_in)

    scores = jax.nn.sigmoid(jnp.dot(normed, router, preferred_element_type=f32))
    chosen = jnp.sum(jnp.where(picked, scores[:, None, :], 0.0), axis=2)
    total = jnp.sum(chosen, axis=1, keepdims=True)
    gates = chosen / total
    slot_gates = jnp.sum(
        jnp.where(first, gates[:, :1], 0.0) + jnp.where(second, gates[:, 1:], 0.0), axis=0
    )
    cot_rows = dot(spread, upstream, ((0,), (0,)))
    d_send = (slot_gates[:, None] * cot_rows).astype(bf16)
    moved_out = exchange(pack(d_send, experts), moved_in)
    d_out = unpack(moved_out)

    pre_gate = dot(expert_in, gate_full, ((1,), (0,)))
    pre_up = dot(expert_in, up_full, ((1,), (0,)))
    sigma = jax.nn.sigmoid(pre_gate)
    active = pre_gate * sigma
    hidden = (active * pre_up).astype(bf16)
    hidden, pre_gate, pre_up = lax.optimization_barrier((hidden, pre_gate, pre_up))
    expert_out = dot(hidden, down_full, ((1,), (0,))).astype(bf16)
    moved_back = exchange(pack(expert_out, experts), moved_out)
    returned = unpack(moved_back)

    sigma = jax.nn.sigmoid(pre_gate)
    active = pre_gate * sigma
    d_hidden = dot(d_out, down_full, ((1,), (1,)))
    d_pre_gate = (d_hidden * pre_up * sigma * (1.0 + pre_gate * (1.0 - sigma))).astype(
        bf16
    )
    d_pre_up = (d_hidden * active).astype(bf16)
    grads = weight_gradients(
        expert_in, d_out, d_pre_gate, d_pre_up, hidden, shards
    )
    mine = lax.psum_scatter(grads, "dp", scatter_dimension=0, tiled=True)
    d_pre_gate, d_pre_up, grads = lax.optimization_barrier((d_pre_gate, d_pre_up, grads))
    d_rows = (
        dot(d_pre_gate, gate_full, ((1,), (1,))) + dot(d_pre_up, up_full, ((1,), (1,)))
    ).astype(bf16)
    moved_rows = exchange(pack(d_rows, experts), moved_back)
    d_back = unpack(moved_rows)
    gain_rows = jnp.sum(d_rows.astype(f32) * expert_in.astype(f32), axis=0) / gain

    cotangent = upstream.astype(f32)
    out_first = dot(take_first, returned, ((1,), (0,)))
    out_second = dot(take_second, returned, ((1,), (0,)))
    mixed = (source + gates[:, :1] * out_first + gates[:, 1:] * out_second).astype(bf16)
    d_gates = jnp.concatenate(
        [
            jnp.sum(cotangent * out_first, axis=1, keepdims=True),
            jnp.sum(cotangent * out_second, axis=1, keepdims=True),
        ],
        axis=1,
    )
    blended = jnp.sum(gates * d_gates, axis=1, keepdims=True)
    d_chosen = (d_gates - blended) / total
    d_logit = d_chosen * chosen * (1.0 - chosen)
    d_logits = jnp.sum(jnp.where(picked, d_logit[:, :, None], 0.0), axis=1)
    d_scored = dot(d_logits, router.astype(f32), ((1,), (1,)), precision=HIGHEST)

    away = jnp.arange(experts, dtype=jnp.uint32)
    owner = ((my_x + away) & (ALONG_X - 1)) * ALONG_Z
    owner = (owner + ((my_z + (away >> 2)) & (ALONG_Z - 1))).astype(jnp.int32)
    d_logits_away = jnp.sum(
        jnp.where(expert_ids[:, :, None] == owner[None, None, :], d_logit[:, :, None], 0.0),
        axis=1,
    )
    part_router = dot(d_logits_away, normed.astype(f32), ((0,), (0,)), precision=HIGHEST)
    part_gain = gain_rows + jnp.sum(d_scored * unit_rows, axis=0)
    piece = width // experts
    choose = (owner[:, None] == columns[None, :]).astype(f32)
    gain_away = dot(choose, part_gain.reshape(experts, piece), ((1,), (0,)), precision=HIGHEST)
    parts = jnp.concatenate(
        [part_router, jnp.pad(gain_away, ((0, 0), (0, 128 - piece)))], axis=1
    )
    parts = lax.optimization_barrier(parts.reshape(ALONG_Z, ALONG_X, width + 128))
    held = parts[0]
    for step in range(1, ALONG_Z):
        held = held + shift_expert(parts[step], 0, step)
    column = held[0]
    for step in range(1, ALONG_X):
        column = column + shift_expert(held[step], step, 0)
    for bit in (1, 2, 4):
        column = column + flip_dp(column, bit)
    near = jnp.stack([column] + [shift_expert(column, -s, 0) for s in range(1, ALONG_X)])
    every = jnp.stack([near] + [shift_expert(near, 0, -s) for s in range(1, ALONG_Z)])
    zero = jnp.uint32(0)
    every = lax.dynamic_slice(
        jnp.concatenate([every, every]),
        ((ALONG_Z - my_z) & (ALONG_Z - 1), zero, zero),
        every.shape,
    ).transpose(1, 0, 2)
    every = lax.dynamic_slice(
        jnp.concatenate([every, every]),
        ((ALONG_X - my_x) & (ALONG_X - 1), zero, zero),
        every.shape,
    ).reshape(experts, width + 128)
    d_router = every[:, :width].T
    d_gain = every[:, width : width + piece].reshape(width)

    d_back, d_router, d_gain, d_scored = lax.optimization_barrier(
        (d_back, d_router, d_gain, d_scored)
    )
    d_normed = dot(spread, d_back, ((1,), (0,))) + d_scored
    d_unit = d_normed * gain
    inner = jnp.mean(d_unit * unit_rows, axis=-1, keepdims=True)
    d_tokens = (cotangent + inverse * (d_unit - unit_rows * inner)).astype(bf16)
    down_pieces = [
        mine[:, 2 * feed + low : 2 * feed + low + mine.shape[0]]
        for low in range(0, feed, mine.shape[0])
    ]
    return (
        mixed,
        d_tokens,
        mine[None, :, :feed],
        mine[None, :, feed : 2 * feed],
        jnp.concatenate(down_pieces, axis=0)[None],
        d_router,
        d_gain,
    )


def solution(mesh):
    return jax.shard_map(
        body,
        mesh=mesh,
        in_specs=(
            P(("dp", "expert"), None),
            P(("dp", "expert"), None),
            P(("dp", "expert"), None),
            P(),
            P(),
            P("expert", "dp", None),
            P("expert", "dp", None),
            P("expert", None, "dp"),
        ),
        out_specs=(
            P(("dp", "expert"), None),
            P(("dp", "expert"), None),
            P("expert", "dp", None),
            P("expert", "dp", None),
            P("expert", None, "dp"),
            P(),
            P(),
        ),
        check_vma=False,
    )
```

```python
import jax
import jax.numpy as jnp
from jax import lax
from jax.experimental import pallas as pl
from jax.experimental.pallas import tpu as pltpu
from jax.sharding import PartitionSpec as P

norm_eps = 1e-06
f32 = jnp.float32
bf16 = jnp.bfloat16
HIGHEST = lax.Precision.HIGHEST


def dot(left, right, dims, **options):
    return lax.dot_general(
        left, right, (dims, ((), ())), preferred_element_type=f32, **options
    )


def pack(rows, experts):
    count, width = rows.shape
    return rows.reshape(experts, count // experts, width // 128, 128)


def unpack(packed):
    return packed.reshape(packed.shape[0] * packed.shape[1], -1)


def exchange(packed, after=None):
    if after is not None:
        packed = lax.optimization_barrier((packed, after))[0]
    return lax.all_to_all(packed, "expert", split_axis=0, concat_axis=0, tiled=True)


def shift_dp(value, step):
    count = lax.axis_size("dp")
    return lax.ppermute(value, "dp", [(i, (i + step) % count) for i in range(count)])


def flip_dp(value):
    count = lax.axis_size("dp")
    return lax.ppermute(value, "dp", [(i, i ^ 1) for i in range(count)])


def gather_by_permutes(block):
    count = lax.axis_size("dp")
    me = lax.axis_index("dp").astype(jnp.uint32)
    rows = block.shape[0]
    before = shift_dp(block, 2)
    after = shift_dp(block, -2)
    far = shift_dp(block, 4)
    full = jnp.zeros((count * rows, block.shape[1]), block.dtype)
    for piece, away in ((block, 0), (before, count - 2), (after, 2), (far, 4)):
        owner = me + away
        for value, index in ((piece, owner), (flip_dp(piece), owner ^ 1)):
            start = (index & (count - 1)) * rows
            full = lax.dynamic_update_slice(full, value, (start, jnp.uint32(0)))
    return full


def weights_kernel(rows_ref, out_ref, gate_ref, up_ref, hidden_ref, grads_ref, columns_ref):
    @pl.when(pl.program_id(0) == 0)
    def _():
        columns_ref[...] = hidden_ref[...].T

    feed = gate_ref.shape[1]
    part = out_ref.shape[1]
    rows = rows_ref[...]
    rows = rows.T
    out = out_ref[...]

    @pl.loop(0, feed // part)
    def _(i):
        at = pl.ds(pl.multiple_of(i * part, part), part)
        grads_ref[:, at] = dot(rows, gate_ref[:, at], ((1,), (0,))).astype(bf16)
        at_up = pl.ds(pl.multiple_of(feed + i * part, part), part)
        grads_ref[:, at_up] = dot(rows, up_ref[:, at], ((1,), (0,))).astype(bf16)
        at_down = pl.ds(pl.multiple_of(2 * feed + i * part, part), part)
        grads_ref[:, at_down] = dot(columns_ref[at, :], out, ((1,), (0,))).astype(bf16)


def weight_gradients(rows, d_out, d_gate, d_up, hidden, parts):
    count, width = rows.shape
    feed = d_gate.shape[1]
    part = width // parts
    whole = pl.BlockSpec((count, feed), lambda p: (0, 0))
    return pl.pallas_call(
        weights_kernel,
        grid=(parts,),
        in_specs=[
            pl.BlockSpec((count, part), lambda p: (0, p)),
            pl.BlockSpec((count, part), lambda p: (0, p)),
            whole,
            whole,
            whole,
        ],
        scratch_shapes=[pltpu.VMEM((feed, count), bf16)],
        out_specs=pl.BlockSpec((part, 3 * feed), lambda p: (p, 0)),
        out_shape=jax.ShapeDtypeStruct((width, 3 * feed), bf16),
        cost_estimate=pl.CostEstimate(
            flops=6 * count * width * feed,
            bytes_accessed=2 * (3 * width * feed + 2 * count * width + 3 * count * feed),
            transcendentals=0,
        ),
        name="weight_gradients",
    )(rows, d_out, d_gate, d_up, hidden)


def body(
    tokens, expert_ids, upstream, gain, router, gate_weight_matrix, up_weight, down_weight
):
    experts = lax.axis_size("expert")
    shards = lax.axis_size("dp")
    tok_rows, width = tokens.shape
    feed = gate_weight_matrix.shape[2]
    capacity = 3 * tok_rows // experts
    slots = experts * capacity

    gate_full = lax.all_gather(gate_weight_matrix[0], "dp", axis=0, tiled=True)
    down_full = lax.all_gather(down_weight[0], "dp", axis=1, tiled=True)
    up_full = gather_by_permutes(up_weight[0])

    columns = jnp.arange(experts, dtype=jnp.int32)
    picked = expert_ids[:, :, None] == columns[None, None, :]
    named = (picked[:, 0] | picked[:, 1]).astype(bf16)
    order = jnp.arange(tok_rows, dtype=jnp.int32)
    earlier = (order[None, :] < order[:, None]).astype(bf16)
    ranks = dot(earlier, named, ((1,), (0,))).astype(jnp.int32)
    place = columns[None, :] * capacity + ranks
    slot_pairs = jnp.sum(jnp.where(picked, place[:, None, :], 0), axis=2)
    slot_of = jnp.arange(slots, dtype=jnp.int32)
    first = slot_of[None, :] == slot_pairs[:, :1]
    second = slot_of[None, :] == slot_pairs[:, 1:]
    take_first = first.astype(bf16)
    take_second = second.astype(bf16)
    spread = (first | second).astype(bf16)

    source = tokens.astype(f32)
    inverse = lax.rsqrt(jnp.mean(source * source, axis=-1, keepdims=True) + norm_eps)
    unit_rows = source * inverse
    normed = (unit_rows * gain).astype(bf16)
    send_rows = dot(spread, normed, ((0,), (0,))).astype(bf16)
    moved_in = exchange(pack(send_rows, experts))
    expert_in = unpack(moved_in)

    scores = jax.nn.sigmoid(jnp.dot(normed, router, preferred_element_type=f32))
    chosen = jnp.sum(jnp.where(picked, scores[:, None, :], 0.0), axis=2)
    total = jnp.sum(chosen, axis=1, keepdims=True)
    gates = chosen / total
    slot_gates = jnp.sum(
        jnp.where(first, gates[:, :1], 0.0) + jnp.where(second, gates[:, 1:], 0.0), axis=0
    )
    cot_rows = dot(spread, upstream, ((0,), (0,)))
    d_send = (slot_gates[:, None] * cot_rows).astype(bf16)
    moved_out = exchange(pack(d_send, experts), moved_in)
    d_out = unpack(moved_out)

    pre_gate = dot(expert_in, gate_full, ((1,), (0,)))
    pre_up = dot(expert_in, up_full, ((1,), (0,)))
    sigma = jax.nn.sigmoid(pre_gate)
    active = pre_gate * sigma
    hidden = (active * pre_up).astype(bf16)
    hidden, pre_gate, pre_up = lax.optimization_barrier((hidden, pre_gate, pre_up))
    expert_out = dot(hidden, down_full, ((1,), (0,))).astype(bf16)
    moved_back = exchange(pack(expert_out, experts), moved_out)
    returned = unpack(moved_back)

    sigma = jax.nn.sigmoid(pre_gate)
    active = pre_gate * sigma
    d_hidden = dot(d_out, down_full, ((1,), (1,)))
    d_pre_gate = (d_hidden * pre_up * sigma * (1.0 + pre_gate * (1.0 - sigma))).astype(
        bf16
    )
    d_pre_up = (d_hidden * active).astype(bf16)
    grads = weight_gradients(
        expert_in, d_out, d_pre_gate, d_pre_up, hidden, shards
    )
    mine = lax.psum_scatter(grads, "dp", scatter_dimension=0, tiled=True)
    d_pre_gate, d_pre_up, grads = lax.optimization_barrier((d_pre_gate, d_pre_up, grads))
    d_rows = (
        dot(d_pre_gate, gate_full, ((1,), (1,))) + dot(d_pre_up, up_full, ((1,), (1,)))
    ).astype(bf16)
    gain_rows = jnp.sum(d_rows.astype(f32) * expert_in.astype(f32), axis=0) / gain

    cotangent = upstream.astype(f32)
    out_first = dot(take_first, returned, ((1,), (0,)))
    out_second = dot(take_second, returned, ((1,), (0,)))
    mixed = (source + gates[:, :1] * out_first + gates[:, 1:] * out_second).astype(bf16)
    d_gates = jnp.concatenate(
        [
            jnp.sum(cotangent * out_first, axis=1, keepdims=True),
            jnp.sum(cotangent * out_second, axis=1, keepdims=True),
        ],
        axis=1,
    )
    blended = jnp.sum(gates * d_gates, axis=1, keepdims=True)
    d_chosen = (d_gates - blended) / total
    d_logit = d_chosen * chosen * (1.0 - chosen)
    d_logits = jnp.sum(jnp.where(picked, d_logit[:, :, None], 0.0), axis=1)
    d_scored = dot(d_logits, router.astype(f32), ((1,), (1,)), precision=HIGHEST)

    part_router = dot(d_logits, normed.astype(f32), ((0,), (0,)), precision=HIGHEST)
    part_gain = gain_rows + jnp.sum(d_scored * unit_rows, axis=0)
    piece = width // experts
    parts = jnp.concatenate(
        [part_router, jnp.pad(part_gain.reshape(experts, piece), ((0, 0), (0, 128 - piece)))],
        axis=1,
    )
    moved_parts = exchange(parts[:, None], moved_back)
    moved_rows = exchange(pack(d_rows, experts), moved_parts)
    column = lax.psum(jnp.sum(moved_parts, axis=0), "dp")
    columns_out = jnp.broadcast_to(column[None], (experts,) + column.shape)
    every = exchange(columns_out, moved_rows)[:, 0]
    d_router = every[:, :width].T
    d_gain = every[:, width : width + piece].reshape(width)

    d_back = unpack(moved_rows)
    d_back, d_scored = lax.optimization_barrier((d_back, d_scored))
    d_normed = dot(spread, d_back, ((1,), (0,))) + d_scored
    d_unit = d_normed * gain
    inner = jnp.mean(d_unit * unit_rows, axis=-1, keepdims=True)
    d_tokens = (cotangent + inverse * (d_unit - unit_rows * inner)).astype(bf16)
    gate_grad = mine[None, :, :feed]
    up_grad = mine[None, :, feed : 2 * feed]
    down_pieces = [
        mine[:, 2 * feed + low : 2 * feed + low + mine.shape[0]]
        for low in range(0, feed, mine.shape[0])
    ]
    down_grad = jnp.concatenate(down_pieces, axis=0)[None]
    return (
        mixed,
        d_tokens,
        gate_grad,
        up_grad,
        down_grad,
        d_router,
        d_gain,
    )


def solution(mesh):
    return jax.shard_map(
        body,
        mesh=mesh,
        in_specs=(
            P(("dp", "expert"), None),
            P(("dp", "expert"), None),
            P(("dp", "expert"), None),
            P(),
            P(),
            P("expert", "dp", None),
            P("expert", "dp", None),
            P("expert", None, "dp"),
        ),
        out_specs=(
            P(("dp", "expert"), None),
            P(("dp", "expert"), None),
            P("expert", "dp", None),
            P("expert", "dp", None),
            P("expert", None, "dp"),
            P(),
            P(),
        ),
        check_vma=False,
    )
```
